32 devices in a mesh: rows: 4 (over z), cols: 8 (over y, x, core).
Axes of the slice: x: 2, y: 2, z: 4, core: 2. Of those that a mesh axis runs over, the one named last changes fastest.
Arguments:
- inputs: bfloat16 [32, 128, 192], P('rows', 'cols'), may hold values from -6 to 6
- step_sizes: bfloat16 [32, 128, 192], P('rows', 'cols'), may hold values from 0.5 to 2
- write_coef: bfloat16 [4, 32, 128, 16], P(None, 'rows', 'cols'), may hold values from -2 to 2
- read_coef: bfloat16 [4, 32, 128, 16], P(None, 'rows', 'cols'), may hold values from -2 to 2
- rate_table: float32 [4, 192, 16], replicated, may hold values from 0.001953125 to 0.08
- skip_gain: float32 [192], replicated, may hold values from 0.5 to 2
- grad_out: bfloat16 [32, 128, 192], P('rows', 'cols'), may hold values from -6 to 6
Outputs:
- grad_inputs: float32 [32, 128, 192], P('rows', 'cols')
- grad_steps: float32 [32, 128, 192], P('rows', 'cols')
- grad_write: float32 [4, 32, 128, 16], P(None, 'rows', 'cols')
- grad_read: float32 [4, 32, 128, 16], P(None, 'rows', 'cols')
- grad_rates: float32 [4, 192, 16], replicated
- grad_skip: float32 [192], replicated
The draws below stay inside these ranges and needn't reach their ends.
All inputs are finite; a program needn't handle non-finite values.
Results may differ from the reference program's by a relative error of at most 0.00045.
Values sent between devices are 32-bit elements; how exact they have to be, the bound alone decides.
No kernel may reach another device: no remote copies, remote signals or barrier semaphores. Data moves between devices by JAX's collectives and lax.ppermute only.
A program may use at most 128 MiB of HBM per device.

```python
import math
import jax
import jax.numpy as jnp
from jax import lax

DI = 192
NS = 16
SCANS = 4
H = 32
W = 128


def shard_levels(key, dims, shards, least, top_value):
    gain, own = 1.0, jax.random.fold_in(key, 6)
    for axis_at, blocks in shards:
        heights = jnp.exp(jax.random.uniform(jax.random.fold_in(own, axis_at), (blocks,), jnp.float32, least / len(shards), top_value / len(shards)))
        gain = gain * jnp.repeat(heights, dims[axis_at] // blocks).reshape([-1 if axis == axis_at else 1 for axis in range(len(dims))])
    return gain


def scatter_about(stream_key, shape, spread, most, pieces=(), dtype=jnp.bfloat16):
    loudness = shard_levels(stream_key, shape, pieces, -0.22, 0.18) if pieces else 1.0
    drawn = jax.random.normal(stream_key, shape, jnp.float32) * spread * loudness
    return jnp.minimum(jnp.maximum(drawn, -most), most).astype(dtype)


def setup_inputs(seed: int = 0) -> dict:
    splits = jax.random.split(jax.random.key(seed), 8)
    inputs = scatter_about(splits[0], (H, W, DI), 1.0, 6.0, ((0, 4), (1, 8)))
    step_sizes = jnp.clip(jnp.exp(math.log(2.0) - 1.3862944 * jax.random.uniform(splits[1], (H, W, DI), jnp.float32) ** shard_levels(splits[1], (H, W, DI), ((0, 4), (1, 8)), -0.2, 0.2)), 0.5, 2.0).astype(jnp.bfloat16)
    write_coef = scatter_about(splits[2], (SCANS, H, W, NS), 0.25, 2.0, ((1, 4), (2, 8)))
    read_coef = scatter_about(splits[3], (SCANS, H, W, NS), 0.25, 2.0, ((1, 4), (2, 8)))
    rate_table = jnp.clip(jnp.exp(jax.random.uniform(splits[4], (SCANS, DI, NS), jnp.float32, math.log(0.001953125), math.log(0.08))), 0.001953125, 0.08)
    skip_gain = jnp.clip(jax.random.uniform(splits[5], (DI,), jnp.float32, 0.5, 2.0), 0.5, 2.0)
    grad_out = scatter_about(splits[6], (H, W, DI), 1.0, 6.0, ((0, 4), (1, 8)))
    return dict(inputs=inputs, step_sizes=step_sizes, write_coef=write_coef, read_coef=read_coef, rate_table=rate_table, skip_gain=skip_gain, grad_out=grad_out)


def line_grads(inputs, steps, write, read, cotan, rates):
    highest = lax.Precision.HIGHEST
    decay = jnp.exp(-steps[..., None] * rates)
    scaled = steps * inputs
    drive = scaled[..., None] * write[:, :, None, :]
    start = jnp.zeros(decay.shape[1:], jnp.float32)

    def forward(state, pair):
        state = pair[0] * state + pair[1]
        return state, state

    _, states = lax.scan(forward, start, (decay, drive))
    before = jnp.concatenate([start[None], states[:-1]], axis=0)
    pulled = cotan[..., None] * read[:, :, None, :]

    def backward(message, pair):
        adjoint = pair[1] + message
        return pair[0] * adjoint, adjoint

    _, adjoint = lax.scan(backward, start, (decay, pulled), reverse=True)
    grad_rd = jnp.einsum("lmdn,lmd->lmn", states, cotan, precision=highest)
    grad_wr = jnp.einsum("lmdn,lmd->lmn", adjoint, scaled, precision=highest)
    through = jnp.einsum("lmdn,lmn->lmd", adjoint, write, precision=highest)
    memory = adjoint * decay * before
    grad_in = through * steps
    grad_st = through * inputs - jnp.einsum("lmdn,dn->lmd", memory, rates, precision=highest)
    grad_rt = -jnp.einsum("lmdn,lmd->dn", memory, steps, precision=highest)
    return grad_in, grad_st, grad_wr, grad_rd, grad_rt


def blocked(inputs, steps, write, read, cotan, rates):
    length = inputs.shape[0]
    line_count = inputs.shape[1]
    block_width = math.gcd(line_count, 16)

    def split(array):
        return array.reshape((length, line_count // block_width, block_width) + array.shape[2:]).swapaxes(0, 1)

    def joined(array):
        return array.swapaxes(0, 1).reshape((length, line_count) + array.shape[3:])

    groups = tuple(split(array) for array in (inputs, steps, write, read, cotan))
    results = lax.map(lambda group: line_grads(group[0], group[1], group[2], group[3], group[4], rates), groups)
    return joined(results[0]), joined(results[1]), joined(results[2]), joined(results[3]), jnp.sum(results[4], axis=0)


def reference(inputs, step_sizes, write_coef, read_coef, rate_table, skip_gain, grad_out):
    values = inputs.astype(jnp.float32)
    steps = step_sizes.astype(jnp.float32)
    writes = write_coef.astype(jnp.float32)
    reads = read_coef.astype(jnp.float32)
    cotan = grad_out.astype(jnp.float32)
    grad_in = skip_gain * cotan
    grad_st = jnp.zeros_like(values)
    write_list = []
    read_list = []
    rate_list = []
    for direction in range(4):
        across = direction < 2
        flipped = direction % 2 == 1

        def arrange(array):
            moved = array.transpose(1, 0, 2) if across else array
            return moved[::-1] if flipped else moved

        def restore(array):
            moved = array[::-1] if flipped else array
            return moved.transpose(1, 0, 2) if across else moved

        parts = blocked(arrange(values), arrange(steps), arrange(writes[direction]), arrange(reads[direction]), arrange(cotan), rate_table[direction])
        grad_in = grad_in + restore(parts[0])
        grad_st = grad_st + restore(parts[1])
        write_list.append(restore(parts[2]))
        read_list.append(restore(parts[3]))
        rate_list.append(parts[4])
    grad_skip = jnp.sum(cotan * values, axis=(0, 1))
    return grad_in, grad_st, jnp.stack(write_list), jnp.stack(read_list), jnp.stack(rate_list), grad_skip
```

```python
import functools
import math

import jax
import jax.numpy as jnp
from jax import lax
from jax.experimental import pallas as pl
from jax.experimental.pallas import tpu as pltpu
from jax.sharding import PartitionSpec as P

LANES = 128
HALF = LANES // 2
SUBS = 8
SLOTS = SUBS // 2
LOG2E = 1.0 / math.log(2.0)
LN2 = math.log(2.0)


def pack_kernel(line_groups, x_ref, dt_ref, dy_ref, wc_ref, rc_ref, row_ref, col_ref):
    f32 = jnp.float32
    height, width = x_ref.shape[:2]
    lines = width // line_groups
    for r in range(height):
        x = x_ref[r].astype(f32)
        dt = dt_ref[r].astype(f32)
        dy = dy_ref[r].astype(f32)
        shared = (
            x[:, :LANES],
            dt[:, :LANES],
            dy[:, :LANES],
            jnp.concatenate([x[:, LANES:], dt[:, LANES:]], axis=-1),
        )
        for at, first in ((0, 0), (1, 2)):
            coefs = [ref[first + i, r].astype(f32) for ref in (wc_ref, rc_ref) for i in range(2)]
            values = shared + (jnp.concatenate([dy[:, LANES:]] + coefs, axis=-1),)
            for i, value in enumerate(values):
                if at == 0:
                    row_ref[r, i] = value
                else:
                    for z in range(line_groups):
                        col_ref[z, i, r * lines : (r + 1) * lines, :] = value[z * lines : (z + 1) * lines]


def slot_rows(t, lines, length, per, tiles, index):
    block = per * lines
    base = (t // per) * (tiles * block) + index * block + (t % per) * lines
    if lines == SLOTS:
        return [(0, SLOTS, pl.ds(base, SLOTS))]
    step = tiles * length * lines
    if lines == 1:
        return [(0, SLOTS, pl.ds(base, SLOTS, stride=step))]
    return [(q * lines, lines, pl.ds(base + q * step, lines)) for q in range(SLOTS // lines)]


def scan_kernel(lines, per, with_skip, buf_ref, tab_ref, out_ref, rate_ref, arr, pre, dec, prior, racc, grd, oa, ob):
    f32 = jnp.float32
    total = buf_ref.shape[0] // 5
    states = tab_ref.shape[0] // 3 * 2
    pairs = states // 2
    tiles = 3 * pairs
    chunks = SLOTS // lines
    length = total // SLOTS
    tile = (SUBS, LANES)
    lane = lax.broadcasted_iota(jnp.int32, tile, 1)
    sub = lax.broadcasted_iota(jnp.int32, tile, 0)
    low = lane < HALF
    first = sub < SLOTS

    def arrange(t, _):
        for i in range(5):
            for base, step in ((0, t), (SLOTS, length - 1 - t)):
                for at, size, rows in slot_rows(step, lines, length, per, 5, i):
                    arr[t, i, base + at : base + at + size, :] = buf_ref[rows, :]
        return 0

    lax.fori_loop(0, length, arrange, 0, unroll=4)

    def prepare(t, total_dt):
        v = [arr[t, i] for i in range(5)]
        turned = pltpu.roll(v[3], HALF, 1)
        x_hi = jnp.where(low, v[3], turned)
        dt_hi = jnp.where(low, turned, v[3])
        dy_hi = jnp.where(low, v[4], pltpu.roll(v[4], HALF, 1))
        coef = jnp.where(first, v[4], pltpu.roll(v[4], LANES - states, 1))
        pre[t, 0] = v[1]
        pre[t, 1] = dt_hi
        pre[t, 2] = v[1] * v[0]
        pre[t, 3] = dt_hi * x_hi
        pre[t, 4] = v[2]
        pre[t, 5] = dy_hi
        pre[t, 6] = coef
        return (total_dt[0] + v[1], total_dt[1] + dt_hi)

    zero = jnp.zeros(tile, f32)
    total_dt = lax.fori_loop(0, length, prepare, (zero, zero), unroll=2)

    def spread(coef, at):
        even = jnp.broadcast_to(coef[:, at : at + 1], tile)
        odd = jnp.broadcast_to(coef[:, at + 1 : at + 2], tile)
        return even, jnp.where(low, even, odd), odd

    def decays(t, kept):
        dts = (pre[t, 0], pre[t, 1], pre[t, 0])
        if kept:
            return [dec[t, i] for i in range(tiles)]
        found = [jnp.exp2(dts[i % 3] * tab_ref[i]) for i in range(tiles)]
        for i in range(tiles):
            dec[t, i] = found[i]
        return found

    b_at = HALF
    c_at = HALF + 2 * states
    zeros = (zero,) * tiles

    if chunks > 1:

        def local_forward(t, h):
            d = decays(t, False)
            u = (pre[t, 2], pre[t, 3], pre[t, 2])
            coef = pre[t, 6]
            out = []
            for p in range(pairs):
                b = spread(coef, b_at + 2 * p)
                for i in range(3):
                    out.append(d[3 * p + i] * h[3 * p + i] + u[i] * b[i])
            return tuple(out)

        ends = lax.fori_loop(0, length, local_forward, zeros)

        def local_backward(s, m):
            t = length - 1 - s
            dy = (pre[t, 4], pre[t, 5], pre[t, 4])
            coef = pre[t, 6]
            out = []
            for p in range(pairs):
                c = spread(coef, c_at + 2 * p)
                for i in range(3):
                    out.append(dec[t, 3 * p + i] * (dy[i] * c[i] + m[3 * p + i]))
            return tuple(out)

        leads = lax.fori_loop(0, length, local_backward, zeros)
        sums = (total_dt[0], total_dt[1], total_dt[0])
        from_above = (sub >= lines) & (sub < SLOTS)
        from_below = (sub >= SLOTS) & (sub < SUBS - lines)
        from_below_a = sub < SLOTS - lines
        from_above_b = sub >= SLOTS + lines

        def shifted(value, down, up):
            return jnp.where(
                down,
                pltpu.roll(value, lines, 0),
                jnp.where(up, pltpu.roll(value, SUBS - lines, 0), 0.0),
            )

        starts = []
        incoming = []
        for i in range(tiles):
            product = jnp.exp2(sums[i % 3] * tab_ref[i])
            state = shifted(ends[i], from_above, from_below)
            message = shifted(leads[i], from_above_b, from_below_a)
            for _ in range(chunks - 2):
                state = shifted(product * state + ends[i], from_above, from_below)
                message = shifted(product * message + leads[i], from_above_b, from_below_a)
            starts.append(state)
            incoming.append(message)
        starts, incoming = tuple(starts), tuple(incoming)
    else:
        starts, incoming = zeros, zeros

    def forward(t, h):
        d = decays(t, chunks > 1)
        u = (pre[t, 2], pre[t, 3], pre[t, 2])
        dy_lo = pre[t, 4]
        dy_hi = pre[t, 5]
        dy_even = jnp.where(low, dy_hi, 0.0)
        dy_odd = jnp.where(low, 0.0, dy_hi)
        coef = pre[t, 6]
        found = zero
        out = []
        for p in range(pairs):
            b = spread(coef, b_at + 2 * p)
            now = []
            for i in range(3):
                j = 3 * p + i
                prior[t, j] = h[j]
                now.append(d[j] * h[j] + u[i] * b[i])
            out.extend(now)
            even = jnp.sum(dy_lo * now[0] + dy_even * now[1], axis=1, keepdims=True)
            odd = jnp.sum(dy_lo * now[2] + dy_odd * now[1], axis=1, keepdims=True)
            found = jnp.where(lane == 2 * states + 2 * p, even, found)
            found = jnp.where(lane == 2 * states + 2 * p + 1, odd, found)
        grd[t] = found
        return tuple(out)

    lax.fori_loop(0, length, forward, starts)

    for i in range(tiles):
        racc[i] = zero

    def backward(s, m):
        t = length - 1 - s
        dt = (pre[t, 0], pre[t, 1], pre[t, 0])
        u_lo = pre[t, 2]
        u_hi = pre[t, 3]
        u_even = jnp.where(low, u_hi, 0.0)
        u_odd = jnp.where(low, 0.0, u_hi)
        dy = (pre[t, 4], pre[t, 5], pre[t, 4])
        coef = pre[t, 6]
        through = [zero, zero]
        memory = [zero, zero]
        found = grd[t]
        out = []
        for p in range(pairs):
            b = spread(coef, b_at + 2 * p)
            c = spread(coef, c_at + 2 * p)
            now = []
            for i in range(3):
                j = 3 * p + i
                k = i % 2
                adjoint = dy[i] * c[i] + m[j]
                now.append(adjoint)
                through[k] = through[k] + adjoint * b[i]
                message = dec[t, j] * adjoint
                kept = message * prior[t, j]
                memory[k] = memory[k] + kept * tab_ref[j]
                racc[j] = racc[j] + kept * dt[i]
                out.append(message)
            even = jnp.sum(u_lo * now[0] + u_even * now[1], axis=1, keepdims=True)
            odd = jnp.sum(u_lo * now[2] + u_odd * now[1], axis=1, keepdims=True)
            found = jnp.where(lane == 2 * p, even, found)
            found = jnp.where(lane == 2 * p + 1, odd, found)
        through_hi = through[1] + pltpu.roll(through[1], HALF, 1)
        memory_hi = memory[1] + pltpu.roll(memory[1], HALF, 1)
        hi = jnp.where(low, through_hi, memory_hi)
        results = (through[0], memory[0], hi, found)
        for n, value in enumerate(results):
            for ref, base, step in ((oa, 0, t), (ob, SLOTS, length - 1 - t)):
                for at, size, rows in slot_rows(step, lines, length, per, 4, n):
                    ref[rows, :] = value[base + at : base + at + size]
        return tuple(out)

    lax.fori_loop(0, length, backward, incoming)

    skip_lo = zero
    skip_hi = zero
    block = per * lines
    for g in range(total // SUBS):
        peer, off = divmod(g * SUBS, block)
        x_lo, dt_lo, dy_lo, mixed, last = (
            buf_ref[pl.ds((peer * 5 + i) * block + off, SUBS), :] for i in range(5)
        )
        cuts = [pl.ds((peer * 4 + i) * block + off, SUBS) for i in range(4)]
        th = oa[cuts[0], :] + ob[cuts[0], :]
        me = oa[cuts[1], :] + ob[cuts[1], :]
        hi = oa[cuts[2], :] + ob[cuts[2], :]
        co = oa[cuts[3], :] + pltpu.roll(ob[cuts[3], :], states, 1)
        out_ref[cuts[0], :] = dt_lo * th
        out_ref[cuts[1], :] = x_lo * th + LN2 * me
        hi_turned = pltpu.roll(hi, HALF, 1)
        mixed_turned = pltpu.roll(mixed, HALF, 1)
        th_hi = jnp.where(low, hi, hi_turned)
        me_hi = jnp.where(low, hi_turned, hi)
        product = mixed_turned * th_hi
        out_ref[cuts[2], :] = jnp.where(low, product, product + LN2 * me_hi)
        out_ref[cuts[3], :] = co
        if with_skip:
            skip_lo = skip_lo + dy_lo * x_lo
            skip_hi = skip_hi + jnp.where(low, last * mixed, 0.0)

    rate_ref[...] = jnp.zeros_like(rate_ref)
    for i in range(tiles):
        acc = racc[i]
        rate_ref[i : i + 1, :] = jnp.sum(jnp.where(first, -acc, 0.0), axis=0, keepdims=True)
        rate_ref[tiles + i : tiles + i + 1, :] = jnp.sum(jnp.where(first, 0.0, -acc), axis=0, keepdims=True)
    if with_skip:
        rate_ref[2 * tiles : 2 * tiles + 1, :] = jnp.sum(skip_lo, axis=0, keepdims=True)
        rate_ref[2 * tiles + 1 : 2 * tiles + 2, :] = jnp.sum(skip_hi, axis=0, keepdims=True)


def scan_lines(buf, table, lines, with_skip):
    f32 = jnp.float32
    peers, _, block, _ = buf.shape
    total = peers * block
    per = block // lines
    tiles = table.shape[0]
    length = total // SLOTS
    rate_rows = 2 * tiles + (SUBS if with_skip else 0)
    out, rates = pl.pallas_call(
        functools.partial(scan_kernel, lines, per, with_skip),
        out_shape=(
            jax.ShapeDtypeStruct((4 * total, LANES), f32),
            jax.ShapeDtypeStruct((rate_rows, LANES), f32),
        ),
        scratch_shapes=[
            pltpu.VMEM((length, 5, SUBS, LANES), f32),
            pltpu.VMEM((length, 7, SUBS, LANES), f32),
            pltpu.VMEM((length, tiles, SUBS, LANES), f32),
            pltpu.VMEM((length, tiles, SUBS, LANES), f32),
            pltpu.VMEM((tiles, SUBS, LANES), f32),
            pltpu.VMEM((length, SUBS, LANES), f32),
            pltpu.VMEM((4 * total, LANES), f32),
            pltpu.VMEM((4 * total, LANES), f32),
        ],
        name="scan_lines",
    )(buf.reshape(-1, LANES), table)
    return out.reshape(peers, 4, block, LANES), rates


def rate_tables(rate_table):
    scans, channels, states = rate_table.shape
    scaled = rate_table.transpose(0, 2, 1) * (-LOG2E)
    lo = scaled[:, :, :LANES].reshape(scans, states // 2, 2, LANES)
    hi = scaled[:, :, LANES:].reshape(scans, states // 2, 1, LANES)
    rows = jnp.concatenate([lo[:, :, :1], hi, lo[:, :, 1:]], axis=2).reshape(scans, -1, LANES)
    paired = rows.reshape(scans // 2, 2, 1, -1, LANES)
    full = jnp.broadcast_to(paired, (scans // 2, 2, SLOTS) + paired.shape[3:])
    return full.reshape(scans // 2, SUBS, -1, LANES).transpose(0, 2, 1, 3)


def rates_back(rows, states):
    packed = rows.reshape(2, states // 2, 3, LANES)
    lo = packed[:, :, 0::2].reshape(2, states, LANES)
    hi = packed[:, :, 1].reshape(2, states, HALF)
    return jnp.concatenate([lo, hi], axis=-1).transpose(0, 2, 1)


def on_device_lines(inputs, step_sizes, write_coef, read_coef, rate_table, skip_gain, grad_out):
    f32 = jnp.float32
    height, width, channels = inputs.shape
    states = write_coef.shape[-1]
    n_cols = lax.axis_size("cols")
    n_rows = lax.axis_size("rows")
    row_lines = height // n_cols
    col_lines = width // n_rows
    send_row, send_col = pl.pallas_call(
        functools.partial(pack_kernel, n_rows),
        out_shape=(
            jax.ShapeDtypeStruct((height, 5, width, LANES), f32),
            jax.ShapeDtypeStruct((n_rows, 5, height * col_lines, LANES), f32),
        ),
        name="pack",
    )(inputs, step_sizes, grad_out, write_coef, read_coef)
    tables = rate_tables(rate_table)
    got_row = lax.all_to_all(send_row, "cols", 0, 0, tiled=True)
    got_col = lax.all_to_all(send_col, "rows", 0, 0, tiled=True)
    out_row, rates_row = scan_lines(got_row, tables[0], row_lines, True)
    out_col, rates_col = scan_lines(got_col, tables[1], col_lines, False)
    back_row = lax.all_to_all(out_row, "cols", 0, 0, tiled=True)
    back_col = lax.all_to_all(out_col, "rows", 0, 0, tiled=True)
    row = back_row.transpose(0, 2, 1, 3).reshape(height, width, 4 * LANES)
    col = back_col.reshape(n_rows, 4, height, col_lines, LANES).transpose(2, 0, 3, 1, 4).reshape(height, width, 4 * LANES)
    both = row + col
    rest = channels - LANES
    grad_in = jnp.concatenate([both[:, :, :LANES], both[:, :, 2 * LANES : 2 * LANES + rest]], axis=-1)
    grad_in = grad_in + skip_gain * grad_out.astype(f32)
    grad_st = jnp.concatenate([both[:, :, LANES : 2 * LANES], both[:, :, 2 * LANES + rest : 3 * LANES]], axis=-1)
    at = 3 * LANES

    def coef(k):
        parts = [a[:, :, at + (2 * k + i) * states : at + (2 * k + i + 1) * states] for a in (row, col) for i in range(2)]
        return jnp.stack(parts)

    every = lax.psum(jnp.concatenate([rates_row, rates_col], axis=0), ("rows", "cols"))
    tiles2 = 2 * tables.shape[1]
    rates = jnp.concatenate([rates_back(every[:tiles2], states), rates_back(every[-tiles2:], states)], axis=0)
    skip = jnp.concatenate([every[tiles2], every[tiles2 + 1, :rest]])
    return grad_in, grad_st, coef(0), coef(1), rates, skip


def prefix(part, axis, combine, identity, reverse):
    count = lax.axis_size(axis)
    place = lax.axis_index(axis)
    ahead = count - 1 - place if reverse else place
    gathered = jax.tree.map(lambda a: lax.all_gather(a, axis), part)
    state = jax.tree.map(lambda a, e: jnp.zeros_like(a) + jnp.asarray(e, a.dtype), part, identity)

    def one(step, state):
        source = count - 1 - step if reverse else step
        return combine(
            state, jax.tree.map(lambda a: lax.dynamic_index_in_dim(a, source, 0, False), gathered)
        )

    return lax.fori_loop(0, ahead, one, state)


def carry_rule():

    def combine(first_pair, second_pair):
        return (first_pair[0] * second_pair[0], second_pair[0] * first_pair[1] + second_pair[1])

    def neutral(final_state):
        return jnp.ones_like(final_state)

    return (combine, neutral)


def chain_cols(totals, finals, combine, first_id, reverse):
    carried = prefix((totals, finals), "cols", combine, (first_id, jnp.zeros_like(finals)), reverse)
    return carried[1]


def chain_rows(totals, finals, combine, first_id, reverse):
    carried = prefix((totals, finals), "rows", combine, (first_id, jnp.zeros_like(finals)), reverse)
    return carried[1]


def arrange(array, direction):
    moved = array.transpose(1, 0, 2) if direction < 2 else array
    return moved[::-1] if direction % 2 == 1 else moved


def restore(array, direction):
    moved = array[::-1] if direction % 2 == 1 else array
    return moved.transpose(1, 0, 2) if direction < 2 else moved


def local_pass(pieces, rates_t):
    values, steps, write, read, cotan = pieces
    empty = jnp.zeros((values.shape[1], rates_t.shape[0], values.shape[2]), jnp.float32)

    def local_forward(carry, slices):
        state, product = carry
        value_row, step_row, write_row = slices
        decay = jnp.exp(-step_row[:, None, :] * rates_t)
        state = decay * state + (step_row * value_row)[:, None, :] * write_row[:, :, None]
        return ((state, product * decay), None)

    (final_state, product), _ = lax.scan(
        local_forward, (empty, jnp.ones_like(empty)), (values, steps, write)
    )

    def local_backward(message, slices):
        step_row, read_row, cotan_row = slices
        decay = jnp.exp(-step_row[:, None, :] * rates_t)
        adjoint = cotan_row[:, None, :] * read_row[:, :, None] + message
        return (decay * adjoint, None)

    outgoing, _ = lax.scan(local_backward, empty, (steps, read, cotan), reverse=True)
    return (product, final_state, outgoing)


def finish(pieces, rates_t, start_state, incoming):
    highest = lax.Precision.HIGHEST
    values, steps, write, read, cotan = pieces

    def finish_forward(state, slices):
        value_row, step_row, write_row = slices
        decay = jnp.exp(-step_row[:, None, :] * rates_t)
        following = decay * state + (step_row * value_row)[:, None, :] * write_row[:, :, None]
        return (following, state)

    _, befores = lax.scan(finish_forward, start_state, (values, steps, write))

    def finish_backward(carry, slices):
        message, rate_acc = carry
        value_row, step_row, write_row, read_row, cotan_row, before = slices
        decay = jnp.exp(-step_row[:, None, :] * rates_t)
        scaled = step_row * value_row
        state = decay * before + scaled[:, None, :] * write_row[:, :, None]
        adjoint = cotan_row[:, None, :] * read_row[:, :, None] + message
        grad_rd = jnp.einsum("mnd,md->mn", state, cotan_row, precision=highest)
        grad_wr = jnp.einsum("mnd,md->mn", adjoint, scaled, precision=highest)
        through = jnp.einsum("mnd,mn->md", adjoint, write_row, precision=highest)
        memory = adjoint * decay * before
        grad_in = through * step_row
        grad_st = through * value_row - jnp.einsum("mnd,nd->md", memory, rates_t, precision=highest)
        rate_acc = rate_acc - jnp.einsum("mnd,md->nd", memory, step_row, precision=highest)
        return ((decay * adjoint, rate_acc), (grad_in, grad_st, grad_wr, grad_rd))

    (_, rate_sum), outputs = lax.scan(
        finish_backward,
        (incoming, jnp.zeros_like(rates_t)),
        (values, steps, write, read, cotan, befores),
        reverse=True,
    )
    return (outputs[0], outputs[1], outputs[2], outputs[3], rate_sum.T)


def on_device_general(inputs, step_sizes, write_coef, read_coef, rate_table, skip_gain, grad_out):
    values = inputs.astype(jnp.float32)
    steps = step_sizes.astype(jnp.float32)
    writes = write_coef.astype(jnp.float32)
    reads = read_coef.astype(jnp.float32)
    cotan = grad_out.astype(jnp.float32)
    grad_in = skip_gain * cotan
    grad_st = jnp.zeros_like(values)
    write_list = [None, None, None, None]
    read_list = [None, None, None, None]
    rate_list = [None, None, None, None]
    for leading in (0, 2):
        trailing = leading + 1
        arranged = {}
        prepared = {}
        rates_of = {}
        for direction in (leading, trailing):
            arranged[direction] = (
                arrange(values, direction),
                arrange(steps, direction),
                arrange(writes[direction], direction),
                arrange(reads[direction], direction),
                arrange(cotan, direction),
            )
            rates_of[direction] = rate_table[direction].T
            prepared[direction] = local_pass(arranged[direction], rates_of[direction])
        starts = {}
        incomings = {}
        chain = chain_cols if leading == 0 else chain_rows
        for direction in (leading, trailing):
            flipped = direction % 2 == 1
            combine, neutral = carry_rule()
            totals, finals, outgoing = prepared[direction]
            starts[direction] = chain(totals, finals, combine, neutral(finals), flipped)
            incomings[direction] = chain(totals, outgoing, combine, neutral(outgoing), not flipped)
        for direction in (leading, trailing):
            parts = finish(
                arranged[direction], rates_of[direction], starts[direction], incomings[direction]
            )
            grad_in = grad_in + restore(parts[0], direction)
            grad_st = grad_st + restore(parts[1], direction)
            write_list[direction] = restore(parts[2], direction)
            read_list[direction] = restore(parts[3], direction)
            rate_list[direction] = parts[4]
    skip_local = jnp.sum(cotan * values, axis=(0, 1))
    rate_local = jnp.stack(rate_list)
    summed_rates, summed_skip = lax.psum((rate_local, skip_local), ("rows", "cols"))
    return (
        grad_in,
        grad_st,
        jnp.stack(write_list),
        jnp.stack(read_list),
        summed_rates,
        summed_skip,
    )


def lines_fit(inputs, write_coef):
    height, width, channels = inputs.shape
    n_cols, n_rows = lax.axis_size("cols"), lax.axis_size("rows")
    states = write_coef.shape[-1]
    if channels != LANES + HALF or 4 * states != HALF or height != n_cols or width % n_rows:
        return False
    for lines, per, peers in ((1, width, n_cols), (width // n_rows, height, n_rows)):
        if SLOTS % lines or (per * peers * lines) % SLOTS:
            return False
        if lines < SLOTS and (per * peers * lines // SLOTS) % per:
            return False
        if (per * lines) % SUBS:
            return False
    return True


def on_device(inputs, step_sizes, write_coef, read_coef, rate_table, skip_gain, grad_out):
    chosen = on_device_lines if lines_fit(inputs, write_coef) else on_device_general
    return chosen(inputs, step_sizes, write_coef, read_coef, rate_table, skip_gain, grad_out)


def solution(mesh):
    in_specs = (
        P("rows", "cols", None),
        P("rows", "cols", None),
        P(None, "rows", "cols", None),
        P(None, "rows", "cols", None),
        P(),
        P(),
        P("rows", "cols", None),
    )
    out_specs = (
        P("rows", "cols", None),
        P("rows", "cols", None),
        P(None, "rows", "cols", None),
        P(None, "rows", "cols", None),
        P(),
        P(),
    )
    return jax.shard_map(
        on_device, mesh=mesh, in_specs=in_specs, out_specs=out_specs, check_vma=False
    )
```

```python
import functools
import math

import jax
import jax.numpy as jnp
from jax import lax
from jax.experimental import pallas as pl
from jax.experimental.pallas import tpu as pltpu
from jax.sharding import PartitionSpec as P

LANES = 128
HALF = LANES // 2
SUBS = 8
SLOTS = SUBS // 2
LOG2E = 1.0 / math.log(2.0)
LN2 = math.log(2.0)
IN_VMEM = pl.BlockSpec(memory_space=pltpu.VMEM)


def pack_kernel(line_groups, me_ref, x_ref, dt_ref, dy_ref, wc_ref, rc_ref, row_ref, *refs):
    col_ref, out_refs = refs[-1], refs[:-1]
    f32 = jnp.float32
    height, width = x_ref.shape[:2]
    lines = width // line_groups
    for r in range(height):
        x = x_ref[r].astype(f32)
        dt = dt_ref[r].astype(f32)
        dy = dy_ref[r].astype(f32)
        shared = (
            x[:, :LANES],
            dt[:, :LANES],
            dy[:, :LANES],
            jnp.concatenate([x[:, LANES:], dt[:, LANES:]], axis=-1),
        )
        for at, first in ((0, 0), (1, 2)):
            coefs = [ref[first + i, r].astype(f32) for i in range(2) for ref in (wc_ref, rc_ref)]
            values = shared + (jnp.concatenate([dy[:, LANES:]] + coefs, axis=-1),)
            for i, value in enumerate(values):
                if at == 0:
                    row_ref[r, i] = value
                else:
                    for z in range(line_groups):
                        col_ref[z, i, r * lines : (r + 1) * lines, :] = value[z * lines : (z + 1) * lines]
    for k, ref in enumerate(out_refs):
        ref[...] = col_ref[me_ref[0] ^ k]


def slot_rows(t, lines, length, per, tiles, index):
    block = per * lines
    base = (t // per) * (tiles * block) + index * block + (t % per) * lines
    if lines == SLOTS:
        return [(0, SLOTS, pl.ds(base, SLOTS))]
    step = tiles * length * lines
    if lines == 1:
        return [(0, SLOTS, pl.ds(base, SLOTS, stride=step))]
    return [(q * lines, lines, pl.ds(base + q * step, lines)) for q in range(SLOTS // lines)]


def scan_kernel(lines, per, peers, split, *refs):
    if split:
        me_ref, *refs = refs
        in_refs, tab_ref, out_refs = refs[:peers], refs[peers], refs[peers + 1 : 2 * peers + 1]
        rate_ref, buf_ref, out_ref, *scratch = refs[2 * peers + 1 :]
        size = in_refs[0].shape[0]
        for k, ref in enumerate(in_refs):
            buf_ref[pl.ds((me_ref[0] ^ k) * size, size), :] = ref[...]
    else:
        buf_ref, tab_ref, out_ref, rate_ref, *scratch = refs
    arr, pre, dec, prior, racc, spr, part, acc4, oa, ob = scratch
    f32 = jnp.float32
    total = buf_ref.shape[0] // 5
    states = tab_ref.shape[0] // 3 * 2
    pairs = states // 2
    tiles = 3 * pairs
    chunks = SLOTS // lines
    length = total // SLOTS
    tile = (SUBS, LANES)
    lane = lax.broadcasted_iota(jnp.int32, tile, 1)
    sub = lax.broadcasted_iota(jnp.int32, tile, 0)
    low = lane < HALF
    first = sub < SLOTS

    def arrange(t, _):
        for i in range(5):
            for base, step in ((0, t), (SLOTS, length - 1 - t)):
                for at, size, rows in slot_rows(step, lines, length, per, 5, i):
                    arr[t, i, base + at : base + at + size, :] = buf_ref[rows, :]
        return 0

    lax.fori_loop(0, length, arrange, 0, unroll=4)

    def prepare(t, total_dt):
        v = [arr[t, i] for i in range(5)]
        turned = pltpu.roll(v[3], HALF, 1)
        x_hi = jnp.where(low, v[3], turned)
        dt_hi = jnp.where(low, turned, v[3])
        dy_hi = jnp.where(low, v[4], pltpu.roll(v[4], HALF, 1))
        coef = jnp.where(first, v[4], pltpu.roll(v[4], LANES - 2 * states, 1))
        pre[t, 0] = v[1]
        pre[t, 1] = dt_hi
        pre[t, 2] = v[1] * v[0]
        pre[t, 3] = dt_hi * x_hi
        pre[t, 4] = v[2]
        pre[t, 5] = dy_hi
        for n in range(2 * states):
            spr[t, n] = jnp.broadcast_to(coef[:, HALF + n : HALF + n + 1], tile)
        return (total_dt[0] + v[1], total_dt[1] + dt_hi)

    zero = jnp.zeros(tile, f32)
    total_dt = lax.fori_loop(0, length, prepare, (zero, zero), unroll=4)

    def spread(t, at):
        even = spr[t, at]
        odd = spr[t, at + 1]
        return even, jnp.where(low, even, odd), odd

    def decays(t, kept):
        dts = (pre[t, 0], pre[t, 1], pre[t, 0])
        if kept:
            return [dec[t, i] for i in range(tiles)]
        found = [jnp.exp2(dts[i % 3] * tab_ref[i]) for i in range(tiles)]
        for i in range(tiles):
            dec[t, i] = found[i]
        return found

    b_at = 0
    c_at = states
    zeros = (zero,) * tiles

    if chunks > 1:

        def local_forward(t, h):
            d = decays(t, False)
            u = (pre[t, 2], pre[t, 3], pre[t, 2])
            out = []
            for p in range(pairs):
                b = spread(t, b_at + 2 * p)
                for i in range(3):
                    out.append(d[3 * p + i] * h[3 * p + i] + u[i] * b[i])
            return tuple(out)

        ends = lax.fori_loop(0, length, local_forward, zeros)

        def local_backward(s, m):
            t = length - 1 - s
            dy = (pre[t, 4], pre[t, 5], pre[t, 4])
            out = []
            for p in range(pairs):
                c = spread(t, c_at + 2 * p)
                for i in range(3):
                    out.append(dec[t, 3 * p + i] * (dy[i] * c[i] + m[3 * p + i]))
            return tuple(out)

        leads = lax.fori_loop(0, length, local_backward, zeros)
        sums = (total_dt[0], total_dt[1], total_dt[0])
        from_above = (sub >= lines) & (sub < SLOTS)
        from_below = (sub >= SLOTS) & (sub < SUBS - lines)
        from_below_a = sub < SLOTS - lines
        from_above_b = sub >= SLOTS + lines

        def shifted(value, down, up):
            return jnp.where(
                down,
                pltpu.roll(value, lines, 0),
                jnp.where(up, pltpu.roll(value, SUBS - lines, 0), 0.0),
            )

        starts = []
        incoming = []
        for i in range(tiles):
            product = jnp.exp2(sums[i % 3] * tab_ref[i])
            state = shifted(ends[i], from_above, from_below)
            message = shifted(leads[i], from_above_b, from_below_a)
            for _ in range(chunks - 2):
                state = shifted(product * state + ends[i], from_above, from_below)
                message = shifted(product * message + leads[i], from_above_b, from_below_a)
            starts.append(state)
            incoming.append(message)
        starts, incoming = tuple(starts), tuple(incoming)
    else:
        starts, incoming = zeros, zeros

    def forward(t, h):
        d = decays(t, chunks > 1)
        u = (pre[t, 2], pre[t, 3], pre[t, 2])
        dy_lo = pre[t, 4]
        dy_hi = pre[t, 5]
        dy_even = jnp.where(low, dy_hi, 0.0)
        dy_odd = jnp.where(low, 0.0, dy_hi)
        out = []
        for p in range(pairs):
            b = spread(t, b_at + 2 * p)
            now = []
            for i in range(3):
                j = 3 * p + i
                prior[t, j] = h[j]
                now.append(d[j] * h[j] + u[i] * b[i])
            out.extend(now)
            part[t, states + 2 * p] = dy_lo * now[0] + dy_even * now[1]
            part[t, states + 2 * p + 1] = dy_lo * now[2] + dy_odd * now[1]
        return tuple(out)

    lax.fori_loop(0, length, forward, starts)

    for i in range(tiles):
        racc[i] = zero

    def backward(s, m):
        t = length - 1 - s
        dt = (pre[t, 0], pre[t, 1], pre[t, 0])
        u_lo = pre[t, 2]
        u_hi = pre[t, 3]
        u_even = jnp.where(low, u_hi, 0.0)
        u_odd = jnp.where(low, 0.0, u_hi)
        dy = (pre[t, 4], pre[t, 5], pre[t, 4])
        through = [zero, zero]
        memory = [zero, zero]
        out = []
        for p in range(pairs):
            b = spread(t, b_at + 2 * p)
            c = spread(t, c_at + 2 * p)
            now = []
            for i in range(3):
                j = 3 * p + i
                k = i % 2
                adjoint = dy[i] * c[i] + m[j]
                now.append(adjoint)
                through[k] = through[k] + adjoint * b[i]
                message = dec[t, j] * adjoint
                kept = message * prior[t, j]
                memory[k] = memory[k] + kept * tab_ref[j]
                racc[j] = racc[j] + kept * dt[i]
                out.append(message)
            part[t, 2 * p] = u_lo * now[0] + u_even * now[1]
            part[t, 2 * p + 1] = u_lo * now[2] + u_odd * now[1]
        acc4[t, 0] = through[0]
        acc4[t, 1] = memory[0]
        acc4[t, 2] = through[1]
        acc4[t, 3] = memory[1]
        return tuple(out)

    lax.fori_loop(0, length, backward, incoming)

    def gather(t, _):
        through_hi = acc4[t, 2]
        memory_hi = acc4[t, 3]
        through_hi = through_hi + pltpu.roll(through_hi, HALF, 1)
        memory_hi = memory_hi + pltpu.roll(memory_hi, HALF, 1)
        found = zero
        for n in range(2 * states):
            at_lane = n if n < states else n + states
            found = jnp.where(lane == at_lane, jnp.sum(part[t, n], axis=1, keepdims=True), found)
        results = (acc4[t, 0], acc4[t, 1], jnp.where(low, through_hi, memory_hi), found)
        for n, value in enumerate(results):
            for ref, base, step in ((oa, 0, t), (ob, SLOTS, length - 1 - t)):
                for at, size, rows in slot_rows(step, lines, length, per, 4, n):
                    ref[rows, :] = value[base + at : base + at + size]
        return 0

    lax.fori_loop(0, length, gather, 0, unroll=4)

    skip_lo = zero
    skip_hi = zero
    block = per * lines
    span = out_ref.shape[0] // (total // block)
    for g in range(total // SUBS):
        peer, off = divmod(g * SUBS, block)
        x_lo, dt_lo, dy_lo, mixed, last = (
            buf_ref[pl.ds((peer * 5 + i) * block + off, SUBS), :] for i in range(5)
        )
        cuts = [pl.ds((peer * 4 + i) * block + off, SUBS) for i in range(4)]
        outs = [pl.ds(peer * span + i * block + off, SUBS) for i in range(4)]
        th = oa[cuts[0], :] + ob[cuts[0], :]
        me = oa[cuts[1], :] + ob[cuts[1], :]
        hi = oa[cuts[2], :] + ob[cuts[2], :]
        co = oa[cuts[3], :] + pltpu.roll(ob[cuts[3], :], states, 1)
        out_ref[outs[0], :] = dt_lo * th
        out_ref[outs[1], :] = x_lo * th + LN2 * me
        hi_turned = pltpu.roll(hi, HALF, 1)
        mixed_turned = pltpu.roll(mixed, HALF, 1)
        th_hi = jnp.where(low, hi, hi_turned)
        me_hi = jnp.where(low, hi_turned, hi)
        product = mixed_turned * th_hi
        out_ref[outs[2], :] = jnp.where(low, product, product + LN2 * me_hi)
        out_ref[outs[3], :] = co
        if not split:
            skip_lo = skip_lo + dy_lo * x_lo
            skip_hi = skip_hi + jnp.where(low, last * mixed, 0.0)

    rate_ref[...] = jnp.zeros_like(rate_ref)
    for i in range(tiles):
        acc = racc[i]
        rate_ref[i : i + 1, :] = jnp.sum(jnp.where(first, -acc, 0.0), axis=0, keepdims=True)
        rate_ref[tiles + i : tiles + i + 1, :] = jnp.sum(jnp.where(first, 0.0, -acc), axis=0, keepdims=True)
    if split:
        size = 4 * block
        for k, ref in enumerate(out_refs):
            ref[...] = out_ref[pl.ds((me_ref[0] ^ k) * size, size), :]
    else:
        rate_ref[2 * tiles : 2 * tiles + 1, :] = jnp.sum(skip_lo, axis=0, keepdims=True)
        rate_ref[2 * tiles + 1 : 2 * tiles + 2, :] = jnp.sum(skip_hi, axis=0, keepdims=True)
        share = rate_ref.shape[0] // peers
        for peer in range(peers):
            at = peer * span + 4 * block
            out_ref[at : at + SUBS, :] = jnp.zeros(tile, f32)
            out_ref[at : at + share, :] = rate_ref[peer * share : (peer + 1) * share, :]


def scan_lines(bufs, table, lines, me=None):
    f32 = jnp.float32
    split = me is not None
    peers = len(bufs) if split else bufs[0].shape[0]
    block = bufs[0].shape[-2]
    total = peers * block
    per = block // lines
    tiles = table.shape[0]
    states = tiles // 3 * 2
    length = total // SLOTS
    scratch = [
        pltpu.VMEM((length, 5, SUBS, LANES), f32),
        pltpu.VMEM((length, 6, SUBS, LANES), f32),
        pltpu.VMEM((length, tiles, SUBS, LANES), f32),
        pltpu.VMEM((length, tiles, SUBS, LANES), f32),
        pltpu.VMEM((tiles, SUBS, LANES), f32),
        pltpu.VMEM((length, 2 * states, SUBS, LANES), f32),
        pltpu.VMEM((length, 2 * states, SUBS, LANES), f32),
        pltpu.VMEM((length, 4, SUBS, LANES), f32),
        pltpu.VMEM((4 * total, LANES), f32),
        pltpu.VMEM((4 * total, LANES), f32),
    ]
    args = [buf.reshape(-1, LANES) for buf in bufs] + [table]
    in_specs = [IN_VMEM] * len(args)
    if split:
        args = [me] + args
        in_specs = [pl.BlockSpec(memory_space=pltpu.SMEM)] + in_specs
        scratch = [pltpu.VMEM((5 * total, LANES), f32), pltpu.VMEM((4 * total, LANES), f32)] + scratch
        out_shape = [jax.ShapeDtypeStruct((4 * block, LANES), f32)] * peers
        out_shape.append(jax.ShapeDtypeStruct((2 * tiles, LANES), f32))
    else:
        out_shape = [
            jax.ShapeDtypeStruct((4 * total + peers * SUBS, LANES), f32),
            jax.ShapeDtypeStruct((2 * tiles + SUBS, LANES), f32),
        ]
    return pl.pallas_call(
        functools.partial(scan_kernel, lines, per, peers, split),
        out_shape=tuple(out_shape),
        scratch_shapes=scratch,
        cost_estimate=pl.CostEstimate(flops=10**10, bytes_accessed=10**6, transcendentals=0),
        in_specs=in_specs,
        out_specs=(IN_VMEM,) * len(out_shape),
        name="scan_lines",
    )(*args)


def unpack_kernel(states, groups, me_ref, row_ref, *refs):
    in_refs = refs[:groups]
    dy_ref, skip_ref, gin_ref, gst_ref, gw_ref, gr_ref, tmp, col_ref = refs[groups:]
    for k, ref in enumerate(in_refs):
        col_ref[me_ref[0] ^ k] = ref[...]
    f32 = jnp.float32
    height, width = dy_ref.shape[:2]
    lines = width // groups
    skip = skip_ref[...]
    for r in range(height):
        for i in range(4):
            for z in range(groups):
                at = (i * height + r) * lines
                tmp[r, i, z * lines : (z + 1) * lines, :] = col_ref[z, at : at + lines, :]
        mine = [row_ref[r, i * width : (i + 1) * width, :] for i in range(4)]
        other = [tmp[r, i] for i in range(4)]
        both = [mine[i] + other[i] for i in range(3)]
        gin = jnp.concatenate([both[0], both[2][:, :HALF]], axis=-1)
        gst = jnp.concatenate([both[1], both[2][:, HALF:]], axis=-1)
        gin_ref[r] = gin + skip * dy_ref[r].astype(f32)
        gst_ref[r] = gst
        for k, value in enumerate((mine[3], mine[3], other[3], other[3])):
            at = (k % 2) * states
            gw_ref[k, r] = value[:, at : at + states]
            gr_ref[k, r] = value[:, at + 2 * states : at + 3 * states]


def rate_tables(rate_table):
    scans, _, states = rate_table.shape
    scaled = rate_table.transpose(0, 2, 1) * (-LOG2E)
    lo = scaled[:, :, :LANES].reshape(scans, states // 2, 2, LANES)
    hi = scaled[:, :, LANES:].reshape(scans, states // 2, 1, LANES)
    rows = jnp.concatenate([lo[:, :, :1], hi, lo[:, :, 1:]], axis=2).reshape(scans, -1, LANES)
    paired = rows.reshape(scans // 2, 2, 1, -1, LANES)
    full = jnp.broadcast_to(paired, (scans // 2, 2, SLOTS) + paired.shape[3:])
    return full.reshape(scans // 2, SUBS, -1, LANES).transpose(0, 2, 1, 3)


def rates_back(rows, states):
    packed = rows.reshape(2, states // 2, 3, LANES)
    lo = packed[:, :, 0::2].reshape(2, states, LANES)
    hi = packed[:, :, 1].reshape(2, states, HALF)
    return jnp.concatenate([lo, hi], axis=-1).transpose(0, 2, 1)


def on_device_lines(inputs, step_sizes, write_coef, read_coef, rate_table, skip_gain, grad_out):
    f32 = jnp.float32
    height, width, channels = inputs.shape
    states = write_coef.shape[-1]
    n_cols = lax.axis_size("cols")
    n_rows = lax.axis_size("rows")
    row_lines = height // n_cols
    col_lines = width // n_rows
    smem = pl.BlockSpec(memory_space=pltpu.SMEM)
    me = lax.axis_index("rows").reshape(1)
    block = height * col_lines

    def swap(parts):
        return [parts[0]] + [
            lax.ppermute(part, "rows", [(i, i ^ k) for i in range(n_rows)])
            for k, part in enumerate(parts)
            if k
        ]

    def all_of(part, axis):
        count = lax.axis_size(axis)
        spread = jnp.broadcast_to(part, (count,) + part.shape)
        return lax.all_to_all(spread, axis, 0, 0, tiled=True)

    send_row, *send_col = pl.pallas_call(
        functools.partial(pack_kernel, n_rows),
        out_shape=(jax.ShapeDtypeStruct((height, 5, width, LANES), f32),)
        + (jax.ShapeDtypeStruct((5, block, LANES), f32),) * n_rows,
        in_specs=[smem] + [IN_VMEM] * 5,
        out_specs=(IN_VMEM,) * (1 + n_rows),
        scratch_shapes=[pltpu.VMEM((n_rows, 5, block, LANES), f32)],
        name="pack",
    )(me, inputs, step_sizes, grad_out, write_coef, read_coef)
    tables = rate_tables(rate_table)
    got_col = swap(send_col)
    got_row = lax.all_to_all(send_row, "cols", 0, 0, tiled=True)
    out_row, rates_row = scan_lines([got_row], tables[0], row_lines)
    back_row = lax.all_to_all(out_row.reshape(n_cols, -1, LANES), "cols", 0, 0, tiled=True)
    *out_col, rates_col = scan_lines(got_col, tables[1], col_lines, me)
    back_col = swap(out_col)
    share = rates_row.shape[0] // n_cols
    mine = jnp.sum(back_row[:, 4 * width :], axis=0)
    partial = all_of(jnp.concatenate([rates_col, mine], axis=0), "rows")
    every = all_of(jnp.sum(partial, axis=0), "cols")
    grad_in, grad_st, grad_wr, grad_rd = pl.pallas_call(
        functools.partial(unpack_kernel, states, n_rows),
        out_shape=(
            jax.ShapeDtypeStruct((height, width, channels), f32),
            jax.ShapeDtypeStruct((height, width, channels), f32),
            jax.ShapeDtypeStruct(write_coef.shape, f32),
            jax.ShapeDtypeStruct(write_coef.shape, f32),
        ),
        scratch_shapes=[
            pltpu.VMEM((height, 4, width, LANES), f32),
            pltpu.VMEM((n_rows, 4 * block, LANES), f32),
        ],
        in_specs=[smem] + [IN_VMEM] * (3 + n_rows),
        out_specs=(IN_VMEM,) * 4,
        name="unpack",
    )(me, back_row, *back_col, grad_out, skip_gain.reshape(1, channels))
    rows = 2 * tables.shape[1]
    rates_b = jnp.sum(every[:, :rows], axis=0)
    rates_a = every[:, rows : rows + share].reshape(-1, LANES)
    grad_rates = jnp.concatenate([rates_back(rates_a[:rows], states), rates_back(rates_b, states)], axis=0)
    skip = jnp.concatenate([rates_a[rows], rates_a[rows + 1, : channels - LANES]])
    return grad_in, grad_st, grad_wr, grad_rd, grad_rates, skip


def prefix(part, axis, combine, identity, reverse):
    count = lax.axis_size(axis)
    place = lax.axis_index(axis)
    ahead = count - 1 - place if reverse else place
    gathered = jax.tree.map(lambda a: lax.all_gather(a, axis), part)
    state = jax.tree.map(lambda a, e: jnp.zeros_like(a) + jnp.asarray(e, a.dtype), part, identity)

    def one(step, state):
        source = count - 1 - step if reverse else step
        return combine(
            state, jax.tree.map(lambda a: lax.dynamic_index_in_dim(a, source, 0, False), gathered)
        )

    return lax.fori_loop(0, ahead, one, state)


def carry_rule():

    def combine(first_pair, second_pair):
        return (first_pair[0] * second_pair[0], second_pair[0] * first_pair[1] + second_pair[1])

    def neutral(final_state):
        return jnp.ones_like(final_state)

    return (combine, neutral)


def chain_cols(totals, finals, combine, first_id, reverse):
    carried = prefix((totals, finals), "cols", combine, (first_id, jnp.zeros_like(finals)), reverse)
    return carried[1]


def chain_rows(totals, finals, combine, first_id, reverse):
    carried = prefix((totals, finals), "rows", combine, (first_id, jnp.zeros_like(finals)), reverse)
    return carried[1]


def arrange(array, direction):
    moved = array.transpose(1, 0, 2) if direction < 2 else array
    return moved[::-1] if direction % 2 == 1 else moved


def restore(array, direction):
    moved = array[::-1] if direction % 2 == 1 else array
    return moved.transpose(1, 0, 2) if direction < 2 else moved


def local_pass(pieces, rates_t):
    values, steps, write, read, cotan = pieces
    empty = jnp.zeros((values.shape[1], rates_t.shape[0], values.shape[2]), jnp.float32)

    def local_forward(carry, slices):
        state, product = carry
        value_row, step_row, write_row = slices
        decay = jnp.exp(-step_row[:, None, :] * rates_t)
        state = decay * state + (step_row * value_row)[:, None, :] * write_row[:, :, None]
        return ((state, product * decay), None)

    (final_state, product), _ = lax.scan(
        local_forward, (empty, jnp.ones_like(empty)), (values, steps, write)
    )

    def local_backward(message, slices):
        step_row, read_row, cotan_row = slices
        decay = jnp.exp(-step_row[:, None, :] * rates_t)
        adjoint = cotan_row[:, None, :] * read_row[:, :, None] + message
        return (decay * adjoint, None)

    outgoing, _ = lax.scan(local_backward, empty, (steps, read, cotan), reverse=True)
    return (product, final_state, outgoing)


def finish(pieces, rates_t, start_state, incoming):
    highest = lax.Precision.HIGHEST
    values, steps, write, read, cotan = pieces

    def finish_forward(state, slices):
        value_row, step_row, write_row = slices
        decay = jnp.exp(-step_row[:, None, :] * rates_t)
        following = decay * state + (step_row * value_row)[:, None, :] * write_row[:, :, None]
        return (following, state)

    _, befores = lax.scan(finish_forward, start_state, (values, steps, write))

    def finish_backward(carry, slices):
        message, rate_acc = carry
        value_row, step_row, write_row, read_row, cotan_row, before = slices
        decay = jnp.exp(-step_row[:, None, :] * rates_t)
        scaled = step_row * value_row
        state = decay * before + scaled[:, None, :] * write_row[:, :, None]
        adjoint = cotan_row[:, None, :] * read_row[:, :, None] + message
        grad_rd = jnp.einsum("mnd,md->mn", state, cotan_row, precision=highest)
        grad_wr = jnp.einsum("mnd,md->mn", adjoint, scaled, precision=highest)
        through = jnp.einsum("mnd,mn->md", adjoint, write_row, precision=highest)
        memory = adjoint * decay * before
        grad_in = through * step_row
        grad_st = through * value_row - jnp.einsum("mnd,nd->md", memory, rates_t, precision=highest)
        rate_acc = rate_acc - jnp.einsum("mnd,md->nd", memory, step_row, precision=highest)
        return ((decay * adjoint, rate_acc), (grad_in, grad_st, grad_wr, grad_rd))

    (_, rate_sum), outputs = lax.scan(
        finish_backward,
        (incoming, jnp.zeros_like(rates_t)),
        (values, steps, write, read, cotan, befores),
        reverse=True,
    )
    return (outputs[0], outputs[1], outputs[2], outputs[3], rate_sum.T)


def on_device_general(inputs, step_sizes, write_coef, read_coef, rate_table, skip_gain, grad_out):
    values = inputs.astype(jnp.float32)
    steps = step_sizes.astype(jnp.float32)
    writes = write_coef.astype(jnp.float32)
    reads = read_coef.astype(jnp.float32)
    cotan = grad_out.astype(jnp.float32)
    grad_in = skip_gain * cotan
    grad_st = jnp.zeros_like(values)
    write_list = [None, None, None, None]
    read_list = [None, None, None, None]
    rate_list = [None, None, None, None]
    for leading in (0, 2):
        trailing = leading + 1
        arranged = {}
        prepared = {}
        rates_of = {}
        for direction in (leading, trailing):
            arranged[direction] = (
                arrange(values, direction),
                arrange(steps, direction),
                arrange(writes[direction], direction),
                arrange(reads[direction], direction),
                arrange(cotan, direction),
            )
            rates_of[direction] = rate_table[direction].T
            prepared[direction] = local_pass(arranged[direction], rates_of[direction])
        starts = {}
        incomings = {}
        chain = chain_cols if leading == 0 else chain_rows
        for direction in (leading, trailing):
            flipped = direction % 2 == 1
            combine, neutral = carry_rule()
            totals, finals, outgoing = prepared[direction]
            starts[direction] = chain(totals, finals, combine, neutral(finals), flipped)
            incomings[direction] = chain(totals, outgoing, combine, neutral(outgoing), not flipped)
        for direction in (leading, trailing):
            parts = finish(
                arranged[direction], rates_of[direction], starts[direction], incomings[direction]
            )
            grad_in = grad_in + restore(parts[0], direction)
            grad_st = grad_st + restore(parts[1], direction)
            write_list[direction] = restore(parts[2], direction)
            read_list[direction] = restore(parts[3], direction)
            rate_list[direction] = parts[4]
    skip_local = jnp.sum(cotan * values, axis=(0, 1))
    rate_local = jnp.stack(rate_list)
    summed_rates, summed_skip = lax.psum((rate_local, skip_local), ("rows", "cols"))
    return (
        grad_in,
        grad_st,
        jnp.stack(write_list),
        jnp.stack(read_list),
        summed_rates,
        summed_skip,
    )


def lines_fit(inputs, write_coef):
    height, width, channels = inputs.shape
    n_cols, n_rows = lax.axis_size("cols"), lax.axis_size("rows")
    states = write_coef.shape[-1]
    if channels != LANES + HALF or 4 * states != HALF or height != n_cols or width % n_rows:
        return False
    for lines, per, peers in ((1, width, n_cols), (width // n_rows, height, n_rows)):
        if SLOTS % lines or (per * peers * lines) % SLOTS:
            return False
        if lines < SLOTS and (per * peers * lines // SLOTS) % per:
            return False
        if (per * lines) % SUBS:
            return False
    return True


def on_device(inputs, step_sizes, write_coef, read_coef, rate_table, skip_gain, grad_out):
    chosen = on_device_lines if lines_fit(inputs, write_coef) else on_device_general
    return chosen(inputs, step_sizes, write_coef, read_coef, rate_table, skip_gain, grad_out)


def solution(mesh):
    in_specs = (
        P("rows", "cols", None),
        P("rows", "cols", None),
        P(None, "rows", "cols", None),
        P(None, "rows", "cols", None),
        P(),
        P(),
        P("rows", "cols", None),
    )
    out_specs = (
        P("rows", "cols", None),
        P("rows", "cols", None),
        P(None, "rows", "cols", None),
        P(None, "rows", "cols", None),
        P(),
        P(),
    )
    return jax.shard_map(
        on_device, mesh=mesh, in_specs=in_specs, out_specs=out_specs, check_vma=False
    )
```

```python
import functools
import math

import jax
import jax.numpy as jnp
from jax import lax
from jax.experimental import pallas as pl
from jax.experimental.pallas import tpu as pltpu
from jax.sharding import PartitionSpec as P

LANES = 128
HALF = LANES // 2
SUBS = 8
SLOTS = SUBS // 2
LOG2E = 1.0 / math.log(2.0)
LN2 = math.log(2.0)
UNROLL = 2
IN_VMEM = pl.BlockSpec(memory_space=pltpu.VMEM)


def near(array):
    return pltpu.with_memory_space_constraint(array, pltpu.VMEM)


def pack_kernel(line_groups, me_ref, x_ref, dt_ref, dy_ref, wc_ref, rc_ref, row_ref, *refs):
    col_ref, out_refs = refs[-1], refs[:-1]
    f32 = jnp.float32
    height, width = x_ref.shape[:2]
    lines = width // line_groups
    for r in range(height):
        x = x_ref[r].astype(f32)
        dt = dt_ref[r].astype(f32)
        dy = dy_ref[r].astype(f32)
        shared = (
            x[:, :LANES],
            dt[:, :LANES],
            dy[:, :LANES],
            jnp.concatenate([x[:, LANES:], dt[:, LANES:]], axis=-1),
        )
        for at, first in ((0, 0), (1, 2)):
            coefs = [ref[first + i, r].astype(f32) for i in range(2) for ref in (wc_ref, rc_ref)]
            values = shared + (jnp.concatenate([dy[:, LANES:]] + coefs, axis=-1),)
            for i, value in enumerate(values):
                if at == 0:
                    row_ref[r, i] = value
                else:
                    for z in range(line_groups):
                        col_ref[z, i, r * lines : (r + 1) * lines, :] = value[z * lines : (z + 1) * lines]
    for k, ref in enumerate(out_refs):
        ref[...] = col_ref[me_ref[0] ^ k]


def slot_rows(t, lines, length, per, tiles, index):
    block = per * lines
    base = (t // per) * (tiles * block) + index * block + (t % per) * lines
    if lines == SLOTS:
        return [(0, SLOTS, pl.ds(base, SLOTS))]
    step = tiles * length * lines
    if lines == 1:
        return [(0, SLOTS, pl.ds(base, SLOTS, stride=step))]
    return [(q * lines, lines, pl.ds(base + q * step, lines)) for q in range(SLOTS // lines)]


def scan_kernel(lines, per, peers, split, *refs):
    if split:
        me_ref, *refs = refs
        in_refs, tab_ref, other_ref, out_refs = refs[:peers], refs[peers], refs[peers + 1], refs[peers + 2 : 2 * peers + 2]
        rate_ref, buf_ref, out_ref, every, *scratch = refs[2 * peers + 2 :]
        size = in_refs[0].shape[0]
        for k, ref in enumerate(in_refs):
            buf_ref[pl.ds((me_ref[0] ^ k) * size, size), :] = ref[...]
    else:
        buf_ref, tab_ref, out_ref, rate_ref, *scratch = refs
    tab, pre, dec, prior, racc, coefs, spr, part, acc4 = scratch
    f32 = jnp.float32
    bf16 = jnp.bfloat16
    total = buf_ref.shape[0] // 5
    states = tab_ref.shape[1]
    pairs = states // 2
    tiles = 3 * pairs
    chunks = SLOTS // lines
    length = total // SLOTS
    tile = (SUBS, LANES)
    lane = lax.broadcasted_iota(jnp.int32, tile, 1)
    sub = lax.broadcasted_iota(jnp.int32, tile, 0)
    low = lane < HALF
    first = sub < SLOTS
    zero = jnp.zeros(tile, f32)

    for i in range(2):
        scaled = tab_ref[i] * (-LOG2E)
        for p in range(pairs):
            even = scaled[2 * p : 2 * p + 1]
            odd = scaled[2 * p + 1 : 2 * p + 2]
            hi = jnp.concatenate([even[:, LANES:], odd[:, LANES:]], axis=1)
            for j, value in enumerate((even[:, :LANES], hi, odd[:, :LANES])):
                tab[3 * p + j, i * SLOTS : (i + 1) * SLOTS, :] = jnp.broadcast_to(value, (SLOTS, LANES))

    for t in range(length):
        for i in range(5):
            for base, step in ((0, t), (SLOTS, length - 1 - t)):
                for at, size, rows in slot_rows(step, lines, length, per, 5, i):
                    pre[t, 4 + i, base + at : base + at + size, :] = buf_ref[rows, :]

    def prepare(t, sums):
        v = [pre[t, 4 + i] for i in range(5)]
        turned = pltpu.roll(v[3], HALF, 1)
        last = pltpu.roll(v[4], HALF, 1)
        x_hi = jnp.where(low, v[3], turned)
        dt_hi = jnp.where(low, turned, v[3])
        dy_hi = jnp.where(low, v[4], last)
        coefs[pl.ds(pl.multiple_of(t * SUBS, SUBS), SUBS), :] = jnp.where(
            first, last, pltpu.roll(v[4], HALF - 2 * states, 1)
        )
        pre[t, 0] = v[1]
        pre[t, 1] = dt_hi
        pre[t, 2] = v[1] * v[0]
        pre[t, 3] = dt_hi * x_hi
        pre[t, 5] = x_hi
        pre[t, 6] = v[2]
        pre[t, 7] = dy_hi
        sums = (sums[0] + v[1], sums[1] + dt_hi) + sums[2:]
        if split:
            return sums
        return sums[:2] + (sums[2] + v[2] * v[0], sums[3] + dy_hi * x_hi)

    sums = lax.fori_loop(0, length, prepare, (zero,) * (2 if split else 4), unroll=8)

    narrow = coefs[:, : 2 * states].astype(bf16)
    which = lax.broadcasted_iota(jnp.int32, (2 * states, LANES), 0)
    for n in range(0, 2 * states, 2):
        pick = jnp.concatenate([(which == n).astype(f32), (which == n + 1).astype(f32)], axis=1)
        spread_two = jnp.dot(narrow, pick.astype(bf16), preferred_element_type=f32)
        spr[n] = spread_two[:, :LANES]
        spr[n + 1] = spread_two[:, LANES:]

    def at_step(t):
        return pl.ds(pl.multiple_of(t * SUBS, SUBS), SUBS)

    def spread(t, at):
        even = spr[at, at_step(t)]
        odd = spr[at + 1, at_step(t)]
        return even, jnp.where(low, even, odd), odd

    def decays(t, kept):
        dts = (pre[t, 0], pre[t, 1], pre[t, 0])
        if kept:
            return [dec[t, i] for i in range(tiles)]
        found = [jnp.exp2(dts[i % 3] * tab[i]) for i in range(tiles)]
        for i in range(tiles):
            dec[t, i] = found[i]
        return found

    zeros = (zero,) * tiles

    if chunks > 1:

        def local_forward(t, h):
            d = decays(t, False)
            u = (pre[t, 2], pre[t, 3], pre[t, 2])
            out = []
            for p in range(pairs):
                b = spread(t, 2 * p)
                for i in range(3):
                    out.append(d[3 * p + i] * h[3 * p + i] + u[i] * b[i])
            return tuple(out)

        ends = lax.fori_loop(0, length, local_forward, zeros, unroll=UNROLL)

        def local_backward(s, m):
            t = length - 1 - s
            dy = (pre[t, 6], pre[t, 7], pre[t, 6])
            out = []
            for p in range(pairs):
                c = spread(t, states + 2 * p)
                for i in range(3):
                    out.append(dec[t, 3 * p + i] * (dy[i] * c[i] + m[3 * p + i]))
            return tuple(out)

        leads = lax.fori_loop(0, length, local_backward, zeros, unroll=UNROLL)
        from_above = (sub >= lines) & (sub < SLOTS)
        from_below = (sub >= SLOTS) & (sub < SUBS - lines)
        from_below_a = sub < SLOTS - lines
        from_above_b = sub >= SLOTS + lines

        def shifted(value, down, up):
            return jnp.where(
                down,
                pltpu.roll(value, lines, 0),
                jnp.where(up, pltpu.roll(value, SUBS - lines, 0), 0.0),
            )

        starts = []
        incoming = []
        for i in range(tiles):
            product = jnp.exp2(sums[i % 3 % 2] * tab[i])
            state = shifted(ends[i], from_above, from_below)
            message = shifted(leads[i], from_above_b, from_below_a)
            for _ in range(chunks - 2):
                state = shifted(product * state + ends[i], from_above, from_below)
                message = shifted(product * message + leads[i], from_above_b, from_below_a)
            starts.append(state)
            incoming.append(message)
        starts, incoming = tuple(starts), tuple(incoming)
    else:
        starts, incoming = zeros, zeros

    def forward(t, h):
        d = decays(t, chunks > 1)
        u = (pre[t, 2], pre[t, 3], pre[t, 2])
        dy_lo = pre[t, 6]
        dy_hi = pre[t, 7]
        dy_even = jnp.where(low, dy_hi, 0.0)
        dy_odd = jnp.where(low, 0.0, dy_hi)
        out = []
        for p in range(pairs):
            b = spread(t, 2 * p)
            now = []
            for i in range(3):
                j = 3 * p + i
                prior[t, j] = h[j]
                now.append(d[j] * h[j] + u[i] * b[i])
            out.extend(now)
            part[states + 2 * p, at_step(t)] = dy_lo * now[0] + dy_even * now[1]
            part[states + 2 * p + 1, at_step(t)] = dy_lo * now[2] + dy_odd * now[1]
        return tuple(out)

    lax.fori_loop(0, length, forward, starts, unroll=UNROLL)

    for i in range(tiles):
        racc[i] = zero

    def backward(s, m):
        t = length - 1 - s
        dt = (pre[t, 0], pre[t, 1], pre[t, 0])
        u_lo = pre[t, 2]
        u_hi = pre[t, 3]
        u_even = jnp.where(low, u_hi, 0.0)
        u_odd = jnp.where(low, 0.0, u_hi)
        dy = (pre[t, 6], pre[t, 7], pre[t, 6])
        through = [zero, zero]
        memory = [zero, zero]
        out = []
        for p in range(pairs):
            b = spread(t, 2 * p)
            c = spread(t, states + 2 * p)
            now = []
            for i in range(3):
                j = 3 * p + i
                k = i % 2
                adjoint = dy[i] * c[i] + m[j]
                now.append(adjoint)
                through[k] = through[k] + adjoint * b[i]
                message = dec[t, j] * adjoint
                kept = message * prior[t, j]
                memory[k] = memory[k] + kept * tab[j]
                racc[j] = racc[j] + kept * dt[i]
                out.append(message)
            part[2 * p, at_step(t)] = u_lo * now[0] + u_even * now[1]
            part[2 * p + 1, at_step(t)] = u_lo * now[2] + u_odd * now[1]
        acc4[t, 0] = through[0]
        acc4[t, 1] = memory[0]
        acc4[t, 2] = through[1]
        acc4[t, 3] = memory[1]
        return tuple(out)

    lax.fori_loop(0, length, backward, incoming, unroll=UNROLL)

    row_lane = lax.broadcasted_iota(jnp.int32, (1, LANES), 1)
    found = jnp.zeros((length * SUBS, LANES), f32)
    for n in range(2 * states):
        target = n if n < states else n + states
        ones = ((row_lane == target) | (row_lane == target + states)).astype(f32).astype(bf16)
        ones = jnp.broadcast_to(ones, (2 * LANES, LANES))
        value = part[n]
        big = value.astype(bf16)
        small = (value - big.astype(f32)).astype(bf16)
        found = found + jnp.dot(jnp.concatenate([big, small], axis=1), ones, preferred_element_type=f32)
    coefs[...] = found

    block = per * lines
    mine = ((lane // states) % 2 == 0) == first

    def finished(t):
        th_hi = acc4[t, 2]
        me_hi = acc4[t, 3]
        th_hi = th_hi + pltpu.roll(th_hi, HALF, 1)
        me_hi = me_hi + pltpu.roll(me_hi, HALF, 1)
        th_lo = acc4[t, 0]
        return (
            pre[t, 0] * th_lo,
            pre[t, 4] * th_lo + LN2 * acc4[t, 1],
            jnp.where(low, pre[t, 1] * th_hi, pre[t, 5] * th_hi + LN2 * me_hi),
            jnp.where(mine, coefs[t * SUBS : (t + 1) * SUBS, :], 0.0),
        )

    for t in range(length // 2):
        for n, (a, b) in enumerate(zip(finished(t), finished(length - 1 - t))):
            value = a + pltpu.roll(b, SLOTS, 0)
            for base, step in ((0, t), (SLOTS, length - 1 - t)):
                for at, size, rows in slot_rows(step, lines, length, per, 4, n):
                    out_ref[rows, :] = value[base + at : base + at + size]

    rates = every if split else rate_ref
    offset = other_ref.shape[0] if split else 0
    if split:
        every[...] = jnp.zeros_like(every)
        every[0:offset, :] = other_ref[...]
    else:
        rates[2 * tiles :, :] = zero
    for i in range(tiles):
        acc = racc[i]
        acc = acc + pltpu.roll(acc, 1, 0)
        acc = -(acc + pltpu.roll(acc, 2, 0))
        rates[offset + i : offset + i + 1, :] = acc[SLOTS - 1 : SLOTS]
        rates[offset + tiles + i : offset + tiles + i + 1, :] = acc[SUBS - 1 : SUBS]
    if split:
        size = 4 * block
        for k, ref in enumerate(out_refs):
            ref[...] = out_ref[pl.ds((me_ref[0] ^ k) * size, size), :]
        share = rate_ref.shape[1]
        for j in range(rate_ref.shape[0]):
            rate_ref[j] = every[j * share : (j + 1) * share, :]
    else:
        for i in range(2):
            skip = jnp.where(first, sums[2 + i], 0.0)
            rates[2 * tiles + i : 2 * tiles + i + 1, :] = jnp.sum(skip, axis=0, keepdims=True)


def scan_lines(bufs, table, lines, me=None, other=None, devices=1):
    f32 = jnp.float32
    split = me is not None
    peers = len(bufs) if split else bufs[0].shape[0]
    block = bufs[0].shape[-2]
    total = peers * block
    per = block // lines
    states = table.shape[1]
    tiles = states // 2 * 3
    length = total // SLOTS
    scratch = [
        pltpu.VMEM((tiles, SUBS, LANES), f32),
        pltpu.VMEM((length, 9, SUBS, LANES), f32),
        pltpu.VMEM((length, tiles, SUBS, LANES), f32),
        pltpu.VMEM((length, tiles, SUBS, LANES), f32),
        pltpu.VMEM((tiles, SUBS, LANES), f32),
        pltpu.VMEM((length * SUBS, LANES), f32),
        pltpu.VMEM((2 * states, length * SUBS, LANES), f32),
        pltpu.VMEM((2 * states, length * SUBS, LANES), f32),
        pltpu.VMEM((length, 4, SUBS, LANES), f32),
    ]
    args = [near(buf.reshape(-1, LANES)) for buf in bufs] + [table]
    in_specs = [IN_VMEM] * len(args)
    if split:
        args = [me] + args + [other]
        in_specs = [pl.BlockSpec(memory_space=pltpu.SMEM)] + in_specs + [IN_VMEM]
        share = -(-(2 * tiles + other.shape[0]) // devices)
        scratch = [
            pltpu.VMEM((5 * total, LANES), f32),
            pltpu.VMEM((4 * total, LANES), f32),
            pltpu.VMEM((-(-share * devices // SUBS) * SUBS, LANES), f32),
        ] + scratch
        out_shape = [jax.ShapeDtypeStruct((4 * block, LANES), f32)] * peers
        out_shape.append(jax.ShapeDtypeStruct((devices, share, LANES), f32))
    else:
        out_shape = [
            jax.ShapeDtypeStruct((4 * total, LANES), f32),
            jax.ShapeDtypeStruct((2 * tiles + SUBS, LANES), f32),
        ]
    return pl.pallas_call(
        functools.partial(scan_kernel, lines, per, peers, split),
        out_shape=tuple(out_shape),
        scratch_shapes=scratch,
        cost_estimate=pl.CostEstimate(flops=10**10, bytes_accessed=10**6, transcendentals=0),
        in_specs=in_specs,
        out_specs=(IN_VMEM,) * len(out_shape),
        name="scan_lines",
    )(*args)


def unpack_kernel(states, groups, me_ref, row_ref, *refs):
    in_refs = refs[:groups]
    dy_ref, skip_ref, gin_ref, gst_ref, gw_ref, gr_ref, tmp, col_ref = refs[groups:]
    for k, ref in enumerate(in_refs):
        col_ref[me_ref[0] ^ k] = ref[...]
    f32 = jnp.float32
    height, width = dy_ref.shape[:2]
    lines = width // groups
    skip = skip_ref[...]
    for r in range(height):
        for i in range(4):
            for z in range(groups):
                at = (i * height + r) * lines
                tmp[r, i, z * lines : (z + 1) * lines, :] = col_ref[z, at : at + lines, :]
        mine = [row_ref[r, i * width : (i + 1) * width, :] for i in range(4)]
        other = [tmp[r, i] for i in range(4)]
        both = [mine[i] + other[i] for i in range(3)]
        gin = jnp.concatenate([both[0], both[2][:, :HALF]], axis=-1)
        gst = jnp.concatenate([both[1], both[2][:, HALF:]], axis=-1)
        gin_ref[r] = gin + skip * dy_ref[r].astype(f32)
        gst_ref[r] = gst
        for k, value in enumerate((mine[3], mine[3], other[3], other[3])):
            at = (k % 2) * states
            gw_ref[k, r] = value[:, at : at + states]
            gr_ref[k, r] = value[:, at + 2 * states : at + 3 * states]


def rates_kernel(states, offset, every_ref, rates_ref, skip_ref):
    share = every_ref.shape[1]

    def line(k):
        return every_ref[k // share, k % share : k % share + 1, :]

    tiles = states // 2 * 3
    rest = rates_ref.shape[2] - LANES
    for scan in range(rates_ref.shape[0]):
        for p in range(states // 2):
            base = scan // 2 * offset + scan % 2 * tiles + 3 * p
            hi = line(base + 1)
            for i in range(2):
                n = 2 * p + i
                tail = hi[:, i * rest : (i + 1) * rest]
                rates_ref[scan, n : n + 1, :] = jnp.concatenate([line(base + 2 * i), tail], axis=1)
    skip_ref[...] = jnp.concatenate([line(2 * tiles), line(2 * tiles + 1)[:, :rest]], axis=1)


def on_device_lines(inputs, step_sizes, write_coef, read_coef, rate_table, skip_gain, grad_out):
    f32 = jnp.float32
    height, width, channels = inputs.shape
    states = write_coef.shape[-1]
    n_cols = lax.axis_size("cols")
    n_rows = lax.axis_size("rows")
    row_lines = height // n_cols
    col_lines = width // n_rows
    smem = pl.BlockSpec(memory_space=pltpu.SMEM)
    me = lax.axis_index("rows").reshape(1)
    block = height * col_lines

    def swap(parts):
        return [parts[0]] + [
            lax.ppermute(part, "rows", [(i, i ^ k) for i in range(n_rows)])
            for k, part in enumerate(parts)
            if k
        ]

    send_row, *send_col = pl.pallas_call(
        functools.partial(pack_kernel, n_rows),
        out_shape=(jax.ShapeDtypeStruct((height, 5, width, LANES), f32),)
        + (jax.ShapeDtypeStruct((5, block, LANES), f32),) * n_rows,
        in_specs=[smem] + [IN_VMEM] * 5,
        out_specs=(IN_VMEM,) * (1 + n_rows),
        scratch_shapes=[pltpu.VMEM((n_rows, 5, block, LANES), f32)],
        name="pack",
    )(me, inputs, step_sizes, grad_out, write_coef, read_coef)
    tables = rate_table.transpose(0, 2, 1)
    got_col = swap(send_col)
    got_row = lax.all_to_all(send_row, "cols", 0, 0, tiled=True)
    out_row, rates_row = scan_lines([got_row], tables[:2], row_lines)
    back_row = lax.all_to_all(out_row.reshape(n_cols, -1, LANES), "cols", 0, 0, tiled=True)
    *out_col, terms = scan_lines(got_col, tables[2:], col_lines, me, rates_row, n_rows * n_cols)
    back_col = swap(out_col)
    both = ("rows", "cols")
    partial = lax.all_to_all(terms, both, 0, 0, tiled=True)
    mine = jnp.broadcast_to(jnp.sum(partial, axis=0), partial.shape)
    every = lax.all_to_all(mine, both, 0, 0, tiled=True)
    grad_in, grad_st, grad_wr, grad_rd = pl.pallas_call(
        functools.partial(unpack_kernel, states, n_rows),
        out_shape=(
            jax.ShapeDtypeStruct((height, width, channels), f32),
            jax.ShapeDtypeStruct((height, width, channels), f32),
            jax.ShapeDtypeStruct(write_coef.shape, f32),
            jax.ShapeDtypeStruct(write_coef.shape, f32),
        ),
        scratch_shapes=[
            pltpu.VMEM((height, 4, width, LANES), f32),
            pltpu.VMEM((n_rows, 4 * block, LANES), f32),
        ],
        in_specs=[smem] + [IN_VMEM] * (3 + n_rows),
        out_specs=(IN_VMEM,) * 4,
        name="unpack",
    )(me, near(back_row), *[near(a) for a in back_col], grad_out, skip_gain.reshape(1, channels))
    rates, skip = pl.pallas_call(
        functools.partial(rates_kernel, states, rates_row.shape[0]),
        out_shape=(
            jax.ShapeDtypeStruct(tables.shape, f32),
            jax.ShapeDtypeStruct((1, channels), f32),
        ),
        in_specs=[IN_VMEM],
        out_specs=(IN_VMEM,) * 2,
        name="rates",
    )(near(every))
    grad_rates = rates.transpose(0, 2, 1)
    skip = skip.reshape(channels)
    return grad_in, grad_st, grad_wr, grad_rd, grad_rates, skip


def prefix(part, axis, combine, identity, reverse):
    count = lax.axis_size(axis)
    place = lax.axis_index(axis)
    ahead = count - 1 - place if reverse else place
    gathered = jax.tree.map(lambda a: lax.all_gather(a, axis), part)
    state = jax.tree.map(lambda a, e: jnp.zeros_like(a) + jnp.asarray(e, a.dtype), part, identity)

    def one(step, state):
        source = count - 1 - step if reverse else step
        return combine(
            state, jax.tree.map(lambda a: lax.dynamic_index_in_dim(a, source, 0, False), gathered)
        )

    return lax.fori_loop(0, ahead, one, state)


def carry_rule():

    def combine(first_pair, second_pair):
        return (first_pair[0] * second_pair[0], second_pair[0] * first_pair[1] + second_pair[1])

    def neutral(final_state):
        return jnp.ones_like(final_state)

    return (combine, neutral)


def chain_cols(totals, finals, combine, first_id, reverse):
    carried = prefix((totals, finals), "cols", combine, (first_id, jnp.zeros_like(finals)), reverse)
    return carried[1]


def chain_rows(totals, finals, combine, first_id, reverse):
    carried = prefix((totals, finals), "rows", combine, (first_id, jnp.zeros_like(finals)), reverse)
    return carried[1]


def arrange(array, direction):
    moved = array.transpose(1, 0, 2) if direction < 2 else array
    return moved[::-1] if direction % 2 == 1 else moved


def restore(array, direction):
    moved = array[::-1] if direction % 2 == 1 else array
    return moved.transpose(1, 0, 2) if direction < 2 else moved


def local_pass(pieces, rates_t):
    values, steps, write, read, cotan = pieces
    empty = jnp.zeros((values.shape[1], rates_t.shape[0], values.shape[2]), jnp.float32)

    def local_forward(carry, slices):
        state, product = carry
        value_row, step_row, write_row = slices
        decay = jnp.exp(-step_row[:, None, :] * rates_t)
        state = decay * state + (step_row * value_row)[:, None, :] * write_row[:, :, None]
        return ((state, product * decay), None)

    (final_state, product), _ = lax.scan(
        local_forward, (empty, jnp.ones_like(empty)), (values, steps, write)
    )

    def local_backward(message, slices):
        step_row, read_row, cotan_row = slices
        decay = jnp.exp(-step_row[:, None, :] * rates_t)
        adjoint = cotan_row[:, None, :] * read_row[:, :, None] + message
        return (decay * adjoint, None)

    outgoing, _ = lax.scan(local_backward, empty, (steps, read, cotan), reverse=True)
    return (product, final_state, outgoing)


def finish(pieces, rates_t, start_state, incoming):
    highest = lax.Precision.HIGHEST
    values, steps, write, read, cotan = pieces

    def finish_forward(state, slices):
        value_row, step_row, write_row = slices
        decay = jnp.exp(-step_row[:, None, :] * rates_t)
        following = decay * state + (step_row * value_row)[:, None, :] * write_row[:, :, None]
        return (following, state)

    _, befores = lax.scan(finish_forward, start_state, (values, steps, write))

    def finish_backward(carry, slices):
        message, rate_acc = carry
        value_row, step_row, write_row, read_row, cotan_row, before = slices
        decay = jnp.exp(-step_row[:, None, :] * rates_t)
        scaled = step_row * value_row
        state = decay * before + scaled[:, None, :] * write_row[:, :, None]
        adjoint = cotan_row[:, None, :] * read_row[:, :, None] + message
        grad_rd = jnp.einsum("mnd,md->mn", state, cotan_row, precision=highest)
        grad_wr = jnp.einsum("mnd,md->mn", adjoint, scaled, precision=highest)
        through = jnp.einsum("mnd,mn->md", adjoint, write_row, precision=highest)
        memory = adjoint * decay * before
        grad_in = through * step_row
        grad_st = through * value_row - jnp.einsum("mnd,nd->md", memory, rates_t, precision=highest)
        rate_acc = rate_acc - jnp.einsum("mnd,md->nd", memory, step_row, precision=highest)
        return ((decay * adjoint, rate_acc), (grad_in, grad_st, grad_wr, grad_rd))

    (_, rate_sum), outputs = lax.scan(
        finish_backward,
        (incoming, jnp.zeros_like(rates_t)),
        (values, steps, write, read, cotan, befores),
        reverse=True,
    )
    return (outputs[0], outputs[1], outputs[2], outputs[3], rate_sum.T)


def on_device_general(inputs, step_sizes, write_coef, read_coef, rate_table, skip_gain, grad_out):
    values = inputs.astype(jnp.float32)
    steps = step_sizes.astype(jnp.float32)
    writes = write_coef.astype(jnp.float32)
    reads = read_coef.astype(jnp.float32)
    cotan = grad_out.astype(jnp.float32)
    grad_in = skip_gain * cotan
    grad_st = jnp.zeros_like(values)
    write_list = [None, None, None, None]
    read_list = [None, None, None, None]
    rate_list = [None, None, None, None]
    for leading in (0, 2):
        trailing = leading + 1
        arranged = {}
        prepared = {}
        rates_of = {}
        for direction in (leading, trailing):
            arranged[direction] = (
                arrange(values, direction),
                arrange(steps, direction),
                arrange(writes[direction], direction),
                arrange(reads[direction], direction),
                arrange(cotan, direction),
            )
            rates_of[direction] = rate_table[direction].T
            prepared[direction] = local_pass(arranged[direction], rates_of[direction])
        starts = {}
        incomings = {}
        chain = chain_cols if leading == 0 else chain_rows
        for direction in (leading, trailing):
            flipped = direction % 2 == 1
            combine, neutral = carry_rule()
            totals, finals, outgoing = prepared[direction]
            starts[direction] = chain(totals, finals, combine, neutral(finals), flipped)
            incomings[direction] = chain(totals, outgoing, combine, neutral(outgoing), not flipped)
        for direction in (leading, trailing):
            parts = finish(
                arranged[direction], rates_of[direction], starts[direction], incomings[direction]
            )
            grad_in = grad_in + restore(parts[0], direction)
            grad_st = grad_st + restore(parts[1], direction)
            write_list[direction] = restore(parts[2], direction)
            read_list[direction] = restore(parts[3], direction)
            rate_list[direction] = parts[4]
    skip_local = jnp.sum(cotan * values, axis=(0, 1))
    rate_local = jnp.stack(rate_list)
    summed_rates, summed_skip = lax.psum((rate_local, skip_local), ("rows", "cols"))
    return (
        grad_in,
        grad_st,
        jnp.stack(write_list),
        jnp.stack(read_list),
        summed_rates,
        summed_skip,
    )


def lines_fit(inputs, write_coef):
    height, width, channels = inputs.shape
    n_cols, n_rows = lax.axis_size("cols"), lax.axis_size("rows")
    states = write_coef.shape[-1]
    if channels != LANES + HALF or 4 * states != HALF or height != n_cols or width % n_rows:
        return False
    for lines, per, peers in ((1, width, n_cols), (width // n_rows, height, n_rows)):
        if SLOTS % lines or (per * peers * lines) % SLOTS:
            return False
        if lines < SLOTS and (per * peers * lines // SLOTS) % per:
            return False
        if (per * lines) % SUBS:
            return False
    return True


def on_device(inputs, step_sizes, write_coef, read_coef, rate_table, skip_gain, grad_out):
    chosen = on_device_lines if lines_fit(inputs, write_coef) else on_device_general
    return chosen(inputs, step_sizes, write_coef, read_coef, rate_table, skip_gain, grad_out)


def solution(mesh):
    in_specs = (
        P("rows", "cols", None),
        P("rows", "cols", None),
        P(None, "rows", "cols", None),
        P(None, "rows", "cols", None),
        P(),
        P(),
        P("rows", "cols", None),
    )
    out_specs = (
        P("rows", "cols", None),
        P("rows", "cols", None),
        P(None, "rows", "cols", None),
        P(None, "rows", "cols", None),
        P(),
        P(),
    )
    return jax.shard_map(
        on_device, mesh=mesh, in_specs=in_specs, out_specs=out_specs, check_vma=False
    )
```
